32 devices in a mesh: gx: 16 (over z, x, core), gy: 2 (over y).
Axes of the slice: x: 2, y: 2, z: 4, core: 2. Of those that a mesh axis runs over, the one named last changes fastest.
Arguments:
- velocity: float32 [3, 14, 1536, 2048], P(None, None, 'gy', 'gx'), may hold values from -6 to 6
- operators: float32 [2, 768, 768], P(None, 'gx'), may hold values from -0.21875 to 0.21875
Outputs:
- tendency: float32 [3, 8, 1536, 2048], P(None, None, 'gy', 'gx')
The draws below stay inside these ranges and needn't reach their ends.
All inputs are finite; a program needn't handle non-finite values.
Results may differ from the reference program's by a relative error of at most 0.000062.
Values sent between devices are 32-bit elements; how exact they have to be, the bound alone decides.
A program may use at most 192 MiB of HBM per device.

```python
import jax
import jax.numpy as jnp
from jax import lax

NY = 1536
NZ = 8
NX = 2048
NZ_RIM = 14


def steps_of(own_key, dims, pieces, least, high):
    def one(position, parts):
        steps = jax.random.uniform(jax.random.fold_in(jax.random.fold_in(own_key, 6), position), (parts,), jnp.float32, least / len(pieces), high / len(pieces))
        return jnp.repeat(jnp.exp(steps), dims[position] // parts).reshape((-1,) + (1,) * (len(dims) - position - 1))

    level = one(*pieces[0])
    for cut in pieces[1:]:
        level = level * one(*cut)
    return level


def centred(own_key, shape, scale, limit, split=(), held_as=jnp.bfloat16):
    entries = jax.random.normal(own_key, shape, jnp.float32) * scale
    if len(split) > 0:
        entries = steps_of(own_key, shape, split, -0.22, 0.18) * entries
    return jnp.clip(entries, min=-limit, max=limit).astype(held_as)


def setup_inputs(seed: int = 0) -> dict:
    key_list = jax.random.split(jax.random.key(seed), 3)
    velocity = centred(key_list[0], (3, NZ_RIM, NY, NX), 1.0, 6.0, ((2, 2), (3, 16)), jnp.float32)
    operators = centred(key_list[1], (2, NY // 2, NY // 2), (NY // 2) ** -0.5, 0.21875, ((1, 16),), jnp.float32)
    return dict(velocity=velocity, operators=operators)


def centered(field, along):
    total = 45.0 * (jnp.roll(field, -1, along) - jnp.roll(field, 1, along))
    total = total - 9.0 * (jnp.roll(field, -2, along) - jnp.roll(field, 2, along))
    total = total + (jnp.roll(field, -3, along) - jnp.roll(field, 3, along))
    return total / 60.0


def window_stencil(field):
    def layer(offset):
        return lax.slice_in_dim(field, 3 + offset, 3 + offset + NZ, axis=0)
    total = 45.0 * (layer(1) - layer(-1)) - 9.0 * (layer(2) - layer(-2)) + (layer(3) - layer(-3))
    return total / 60.0


def reference(velocity, operators):
    halfway = NY // 2

    def component(which):
        full = velocity[which]
        own = full[3:3 + NZ]
        xflux = own * velocity[0, 3:3 + NZ]
        yflux = own * velocity[1, 3:3 + NZ]
        zflux = full * velocity[2]
        upper = yflux[:, :halfway, :]
        lower = jnp.flip(yflux[:, halfway:, :], 1)
        even = upper + lower
        odd = upper - lower
        evenout = jnp.einsum("zkx,kj->zjx", even, operators[0], precision=lax.Precision.HIGHEST)
        oddout = jnp.einsum("zkx,kj->zjx", odd, operators[1], precision=lax.Precision.HIGHEST)
        ydiv = jnp.concatenate([evenout + oddout, jnp.flip(oddout - evenout, 1)], axis=1)
        return -(centered(xflux, 2) + ydiv + window_stencil(zflux))

    return lax.map(component, jnp.arange(3, dtype=jnp.int32))
```

```python
import functools

import jax
import jax.numpy as jnp
import numpy as np
from jax import lax
from jax.experimental import pallas as pl
from jax.experimental.pallas import tpu as pltpu
from jax.sharding import PartitionSpec as P

RIM = 3
WEIGHTS = ((1, 45.0), (2, -9.0), (3, 1.0))
CHUNKS = (2, 2, 2, 1, 1)


def stencil_matrices(width):
    inside = np.zeros((width, width), np.float32)
    rim = np.zeros((8, width), np.float32)
    for m in range(width):
        for step, weight in WEIGHTS:
            for offset, signed in ((step, weight), (-step, -weight)):
                at = m + offset
                if at < 0:
                    rim[at + RIM, m] = signed
                elif at >= width:
                    rim[at - width + RIM, m] = signed
                else:
                    inside[at, m] = signed
    return inside, rim


def split(value):
    high = value.astype(jnp.bfloat16)
    low = (value - high.astype(jnp.float32)).astype(jnp.bfloat16)
    return high, low


def dot(left, right, contract=((1,), (0,)), precision=None):
    return lax.dot_general(
        left, right, (contract, ((), ())),
        preferred_element_type=jnp.float32, precision=precision,
    )


def stencil_kernel(vel_ref, halo_ref, inside_ref, rim_ref, out_ref):
    planes = out_ref.shape[1]
    inside = inside_ref[...]
    rim = rim_ref[...]
    for z in range(planes):
        for i in range(3):
            high, low = split(vel_ref[i, RIM + z] * vel_ref[0, RIM + z])
            total = dot(high, inside) + dot(low, inside)
            edges = halo_ref[i, z] * halo_ref[0, z]
            total += dot(edges, rim, ((0,), (0,)), lax.Precision.HIGHEST)
            for step, weight in WEIGHTS:
                up, down = RIM + z + step, RIM + z - step
                total += weight * (
                    vel_ref[i, up] * vel_ref[2, up] - vel_ref[i, down] * vel_ref[2, down]
                )
            out_ref[i, z] = total * (-1.0 / 60.0)


def stencils(velocity, halo):
    _, held, rows, width = velocity.shape
    planes = held - 2 * RIM
    tile = 128 if rows % 128 == 0 else rows
    inside, rim = stencil_matrices(width)
    return pl.pallas_call(
        stencil_kernel,
        grid=(rows // tile,),
        in_specs=[
            pl.BlockSpec((3, held, tile, width), lambda t: (0, 0, t, 0)),
            pl.BlockSpec((3, planes, 8, tile), lambda t: (0, 0, 0, t)),
            pl.BlockSpec((width, width), lambda t: (0, 0)),
            pl.BlockSpec((8, width), lambda t: (0, 0)),
        ],
        out_specs=pl.BlockSpec((3, planes, tile, width), lambda t: (0, 0, t, 0)),
        out_shape=jax.ShapeDtypeStruct((3, planes, rows, width), jnp.float32),
        compiler_params=pltpu.CompilerParams(vmem_limit_bytes=24 << 20),
        cost_estimate=pl.CostEstimate(
            flops=12 * planes * rows * width * width,
            bytes_accessed=4 * 3 * (held + planes) * rows * width,
            transcendentals=0,
        ),
        name="stencils",
    )(velocity, halo, jnp.asarray(inside, jnp.bfloat16), jnp.asarray(rim))


def flip_or_same(size, flipped):
    row = lax.broadcasted_iota(jnp.int32, (size, size), 0)
    column = lax.broadcasted_iota(jnp.int32, (size, size), 1)
    wanted = jnp.where(flipped == 1, size - 1 - column, column)
    return jnp.where(row == wanted, 1.0, 0.0).astype(jnp.bfloat16)


def weights_kernel(flags, piece_ref, high_ref, low_ref):
    entry = pl.program_id(0) * 4
    block, same, flip_in, flip_out = (flags[entry + k] for k in range(4))
    depth, tile = high_ref.shape[2], high_ref.shape[1]
    at = pl.ds(pl.multiple_of(block * depth, 8), depth)
    even, odd = piece_ref[0, at, :], piece_ref[1, at, :]
    combined = even + jnp.where(same == 1, odd, -odd)
    combined = jnp.where(flip_out == 1, combined, -combined)
    turn_in = flip_or_same(depth, flip_in)
    turn_out = flip_or_same(tile, flip_out)
    for part, out_ref in zip(split(combined), (high_ref, low_ref)):
        turned = dot(part, turn_in, ((0,), (0,))).astype(jnp.bfloat16)
        out_ref[0] = dot(turn_out, turned).astype(jnp.bfloat16)


def column_weights(piece, position, count):
    _, halfway, rows = piece.shape
    tile = 256 if rows % 256 == 0 else rows
    tiles = rows // tile
    source = lax.rem(position + jnp.arange(count, dtype=jnp.int32), count)
    low_half = source >= count // 2
    mine = position >= count // 2
    flags = jnp.stack(
        [
            jnp.where(low_half, count - 1 - source, source),
            (low_half == mine).astype(jnp.int32),
            low_half.astype(jnp.int32),
            jnp.broadcast_to(mine, (count,)).astype(jnp.int32),
        ],
        axis=1,
    ).reshape(-1)
    shape = jax.ShapeDtypeStruct((count, rows, rows), jnp.bfloat16)
    out_spec = pl.BlockSpec((1, tile, rows), lambda s, g, flags: (s, g, 0))
    return pl.pallas_call(
        weights_kernel,
        grid_spec=pltpu.PrefetchScalarGridSpec(
            num_scalar_prefetch=1,
            grid=(count, tiles),
            in_specs=[
                pl.BlockSpec(
                    (2, halfway, tile),
                    lambda s, g, flags: (
                        0, 0, jnp.where(flags[s * 4 + 3] == 1, tiles - 1 - g, g)
                    ),
                )
            ],
            out_specs=[out_spec, out_spec],
        ),
        out_shape=[shape, shape],
        compiler_params=pltpu.CompilerParams(vmem_limit_bytes=24 << 20),
        cost_estimate=pl.CostEstimate(
            flops=8 * count * rows * rows * rows,
            bytes_accessed=count * rows * (8 * halfway + 4 * rows),
            transcendentals=0,
        ),
        name="weights",
    )(flags, piece)


def column_kernel(first, count, acc_ref, high_ref, low_ref, *refs):
    *lines, out_ref = refs
    total = None
    for s in range(count):
        line = lines[s]
        v = line[1, 0]
        high, low = split(jnp.concatenate([line[i, 0] * v for i in range(3)], axis=1))
        w_high, w_low = high_ref[first + s], low_ref[first + s]
        term = dot(w_high, high) + (dot(w_high, low) + dot(w_low, high))
        total = term if total is None else total + term
    width = out_ref.shape[3]
    for i in range(3):
        out_ref[i, 0] = acc_ref[i, 0] + total[:, i * width:(i + 1) * width]


def add_column(acc, weights, first, lines, offset, start, planes):
    high, low = weights
    _, _, rows, width = acc.shape
    count = len(lines)
    block = (3, 1, rows, width)
    held = pl.BlockSpec(block, lambda z: (0, start + z, 0, 0))
    whole = pl.BlockSpec(high.shape, lambda z: (0, 0, 0), pipeline_mode=pl.Buffered(1))
    if count == 1:
        whole = pl.BlockSpec(
            (1,) + high.shape[1:], lambda z: (first, 0, 0), pipeline_mode=pl.Buffered(1)
        )
        first_in_block = 0
    else:
        first_in_block = first
    return pl.pallas_call(
        functools.partial(column_kernel, first_in_block, count),
        grid=(planes,),
        in_specs=[held, whole, whole]
        + [pl.BlockSpec(block, lambda z: (0, offset + z, 0, 0))] * count,
        out_specs=held,
        out_shape=jax.ShapeDtypeStruct(acc.shape, acc.dtype),
        input_output_aliases={0: 0},
        compiler_params=pltpu.CompilerParams(vmem_limit_bytes=32 << 20),
        cost_estimate=pl.CostEstimate(
            flops=18 * planes * count * rows * rows * width,
            bytes_accessed=4 * 3 * planes * (2 + count) * rows * width + 4 * count * rows * rows,
            transcendentals=0,
        ),
        name="column",
    )(acc, high, low, *lines)


def around(count, step):
    return [((i + step) % count, i) for i in range(count)]


def shards(velocity, operators):
    _, held, rows, width = velocity.shape
    planes = held - 2 * RIM
    ring = lax.axis_size("gx")
    count = lax.axis_size("gy")
    position = lax.axis_index("gy")

    starts, sizes, at = [], [], 0
    for size in CHUNKS:
        size = min(size, planes - at)
        if size > 0:
            starts.append(at)
            sizes.append(size)
            at += size
    if at < planes:
        starts.append(at)
        sizes.append(planes - at)
    arrived = []
    for start, size in zip(starts, sizes):
        part = lax.slice_in_dim(velocity, RIM + start, RIM + start + size, axis=1)
        arrived.append([lax.ppermute(part, "gy", around(count, s)) for s in range(1, count)])

    inner = lax.slice_in_dim(velocity, RIM, RIM + planes, axis=1)
    left = jnp.swapaxes(lax.slice_in_dim(inner, width - RIM, width, axis=3), 2, 3)
    right = jnp.swapaxes(lax.slice_in_dim(inner, 0, RIM, axis=3), 2, 3)
    left = lax.ppermute(left, "gx", around(ring, ring - 1))
    right = lax.ppermute(right, "gx", around(ring, 1))
    nothing = jnp.zeros((3, planes, 8 - 2 * RIM, rows), jnp.float32)
    halo = jnp.concatenate([left, right, nothing], axis=2)

    block = jnp.where(position >= count // 2, count - 1 - position, position)
    own_columns = lax.dynamic_slice_in_dim(operators, block * rows, rows, axis=2)
    piece = lax.all_gather(own_columns, "gx", axis=1, tiled=True)
    weights = column_weights(piece, position, count)

    acc = stencils(velocity, halo)
    acc = add_column(acc, weights, 0, [velocity], RIM, 0, planes)
    for start, size, lines in zip(starts, sizes, arrived):
        acc = add_column(acc, weights, 1, lines, 0, start, size)
    return acc


def solution(mesh):
    placed = (P(None, None, "gy", "gx"), P(None, "gx", None))
    return jax.shard_map(
        shards, mesh=mesh, in_specs=placed, out_specs=P(None, None, "gy", "gx"), check_vma=False
    )
```

```python
import functools

import jax
import jax.numpy as jnp
import numpy as np
from jax import lax
from jax.experimental import pallas as pl
from jax.experimental.pallas import tpu as pltpu
from jax.sharding import PartitionSpec as P

RIM = 3
WEIGHTS = ((1, 45.0), (2, -9.0), (3, 1.0))
CHUNKS = (1, 6, 1)


def stencil_matrices(width):
    inside = np.zeros((width, width), np.float32)
    rim = np.zeros((8, width), np.float32)
    for m in range(width):
        for step, weight in WEIGHTS:
            for offset, signed in ((step, weight), (-step, -weight)):
                at = m + offset
                if at < 0:
                    rim[at + RIM, m] = signed
                elif at >= width:
                    rim[at - width + RIM, m] = signed
                else:
                    inside[at, m] = signed
    return inside, rim


def split(value):
    high = value.astype(jnp.bfloat16)
    low = (value - high.astype(jnp.float32)).astype(jnp.bfloat16)
    return high, low


def dot(left, right, contract=((1,), (0,)), precision=None):
    return lax.dot_general(
        left, right, (contract, ((), ())),
        preferred_element_type=jnp.float32, precision=precision,
    )


def stencil_kernel(vel_ref, halo_ref, inside_ref, rim_ref, out_ref):
    planes = out_ref.shape[1]
    inside = inside_ref[...]
    rim = rim_ref[...]
    for z in range(planes):
        for i in range(3):
            high, low = split(vel_ref[i, RIM + z] * vel_ref[0, RIM + z])
            total = dot(high, inside) + dot(low, inside)
            edges = halo_ref[i, z] * halo_ref[0, z]
            total += dot(edges, rim, ((0,), (0,)), lax.Precision.HIGHEST)
            for step, weight in WEIGHTS:
                up, down = RIM + z + step, RIM + z - step
                total += weight * (
                    vel_ref[i, up] * vel_ref[2, up] - vel_ref[i, down] * vel_ref[2, down]
                )
            out_ref[i, z] = total * (-1.0 / 60.0)


def stencils(velocity, halo):
    _, held, rows, width = velocity.shape
    planes = held - 2 * RIM
    tile = 128 if rows % 128 == 0 else rows
    inside, rim = stencil_matrices(width)
    return pl.pallas_call(
        stencil_kernel,
        grid=(rows // tile,),
        in_specs=[
            pl.BlockSpec((3, held, tile, width), lambda t: (0, 0, t, 0)),
            pl.BlockSpec((3, planes, 8, tile), lambda t: (0, 0, 0, t)),
            pl.BlockSpec((width, width), lambda t: (0, 0)),
            pl.BlockSpec((8, width), lambda t: (0, 0)),
        ],
        out_specs=pl.BlockSpec((3, planes, tile, width), lambda t: (0, 0, t, 0)),
        out_shape=jax.ShapeDtypeStruct((3, planes, rows, width), jnp.float32),
        compiler_params=pltpu.CompilerParams(vmem_limit_bytes=24 << 20),
        cost_estimate=pl.CostEstimate(
            flops=12 * planes * rows * width * width,
            bytes_accessed=4 * 3 * (held + planes) * rows * width,
            transcendentals=0,
        ),
        name="stencils",
    )(velocity, halo, jnp.asarray(inside, jnp.bfloat16), jnp.asarray(rim))


def flip_or_same(size, flipped):
    row = lax.broadcasted_iota(jnp.int32, (size, size), 0)
    column = lax.broadcasted_iota(jnp.int32, (size, size), 1)
    wanted = jnp.where(flipped == 1, size - 1 - column, column)
    return jnp.where(row == wanted, 1.0, 0.0).astype(jnp.bfloat16)


def weights_kernel(flags, piece_ref, high_ref, low_ref):
    entry = pl.program_id(0) * 4
    block, same, flip_in, flip_out = (flags[entry + k] for k in range(4))
    depth, tile = high_ref.shape[2], high_ref.shape[1]
    strip = piece_ref.shape[3]
    pairs = depth // (2 * strip)
    even, odd = (
        jnp.concatenate(
            [piece_ref[core, block * pairs + r, c] for r in range(pairs) for core in range(2)],
            axis=0,
        )
        for c in range(2)
    )
    combined = even + jnp.where(same == 1, odd, -odd)
    combined = jnp.where(flip_out == 1, combined, -combined)
    turn_in = flip_or_same(depth, flip_in)
    turn_out = flip_or_same(tile, flip_out)
    for part, out_ref in zip(split(combined), (high_ref, low_ref)):
        turned = dot(part, turn_in, ((0,), (0,))).astype(jnp.bfloat16)
        out_ref[0] = dot(turn_out, turned).astype(jnp.bfloat16)


def column_weights(piece, position, count):
    _, pairs, _, strip, rows = piece.shape
    halfway = 2 * pairs * strip
    tile = 256 if rows % 256 == 0 else rows
    tiles = rows // tile
    source = lax.rem(position + jnp.arange(count, dtype=jnp.int32), count)
    low_half = source >= count // 2
    mine = position >= count // 2
    flags = jnp.stack(
        [
            jnp.where(low_half, count - 1 - source, source),
            (low_half == mine).astype(jnp.int32),
            low_half.astype(jnp.int32),
            jnp.broadcast_to(mine, (count,)).astype(jnp.int32),
        ],
        axis=1,
    ).reshape(-1)
    shape = jax.ShapeDtypeStruct((count, rows, rows), jnp.bfloat16)
    out_spec = pl.BlockSpec((1, tile, rows), lambda s, g, flags: (s, g, 0))
    return pl.pallas_call(
        weights_kernel,
        grid_spec=pltpu.PrefetchScalarGridSpec(
            num_scalar_prefetch=1,
            grid=(count, tiles),
            in_specs=[
                pl.BlockSpec(
                    (2, pairs, 2, strip, tile),
                    lambda s, g, flags: (
                        0, 0, 0, 0, jnp.where(flags[s * 4 + 3] == 1, tiles - 1 - g, g)
                    ),
                )
            ],
            out_specs=[out_spec, out_spec],
        ),
        out_shape=[shape, shape],
        compiler_params=pltpu.CompilerParams(vmem_limit_bytes=24 << 20),
        cost_estimate=pl.CostEstimate(
            flops=8 * count * rows * rows * rows,
            bytes_accessed=count * rows * (8 * halfway + 4 * rows),
            transcendentals=0,
        ),
        name="weights",
    )(flags, piece)


def column_kernel(first, count, acc_ref, high_ref, low_ref, *refs):
    *lines, out_ref = refs
    total = None
    for s in range(count):
        line = lines[s]
        v = line[1, 0]
        high, low = split(jnp.concatenate([line[i, 0] * v for i in range(3)], axis=1))
        w_high, w_low = high_ref[first + s], low_ref[first + s]
        term = dot(w_high, high) + (dot(w_high, low) + dot(w_low, high))
        total = term if total is None else total + term
    width = out_ref.shape[3]
    for i in range(3):
        out_ref[i, 0] = acc_ref[i, 0] + total[:, i * width:(i + 1) * width]


def add_column(acc, weights, first, lines, offset, start, planes):
    high, low = weights
    _, _, rows, width = acc.shape
    count = len(lines)
    block = (3, 1, rows, width)
    held = pl.BlockSpec(block, lambda z: (0, start + z, 0, 0))
    whole = pl.BlockSpec(high.shape, lambda z: (0, 0, 0), pipeline_mode=pl.Buffered(1))
    if count == 1:
        whole = pl.BlockSpec(
            (1,) + high.shape[1:], lambda z: (first, 0, 0), pipeline_mode=pl.Buffered(1)
        )
        first_in_block = 0
    else:
        first_in_block = first
    return pl.pallas_call(
        functools.partial(column_kernel, first_in_block, count),
        grid=(planes,),
        in_specs=[held, whole, whole]
        + [pl.BlockSpec(block, lambda z: (0, offset + z, 0, 0))] * count,
        out_specs=held,
        out_shape=jax.ShapeDtypeStruct(acc.shape, acc.dtype),
        input_output_aliases={0: 0},
        compiler_params=pltpu.CompilerParams(vmem_limit_bytes=32 << 20),
        cost_estimate=pl.CostEstimate(
            flops=18 * planes * count * rows * rows * width,
            bytes_accessed=4 * 3 * planes * (2 + count) * rows * width + 4 * count * rows * rows,
            transcendentals=0,
        ),
        name="column",
    )(acc, high, low, *lines)


def around(count, step):
    return [((i + step) % count, i) for i in range(count)]


def gather_rows(block, last):
    ring = lax.axis_size("gx")
    me = lax.axis_index("gx")
    if ring & (ring - 1):
        rows = lax.all_gather(block, "gx", axis=0)
        return jnp.swapaxes(rows.reshape((ring // 2, 2) + block.shape), 0, 1), last

    def exchange(held, bit, join):
        other = lax.ppermute(held, "gx", [(i, i ^ (1 << bit)) for i in range(ring)])
        upper = (me >> bit) & 1 == 1
        return join([jnp.where(upper, other, held), jnp.where(upper, held, other)], 0)

    held = block[None]
    for bit in range(1, ring.bit_length() - 1):
        held = exchange(held, bit, jnp.concatenate)
    held, last = lax.optimization_barrier((held, last))
    return exchange(held, 0, jnp.stack), last


def shards(velocity, operators):
    _, held, rows, width = velocity.shape
    planes = held - 2 * RIM
    ring = lax.axis_size("gx")
    count = lax.axis_size("gy")
    position = lax.axis_index("gy")

    cuts, at = [], 0
    for size in CHUNKS:
        if at < planes:
            cuts.append((at, min(size, planes - at)))
            at += size
    if at < planes:
        cuts.append((at, planes - at))

    def plane_range(field, start, size):
        return lax.slice_in_dim(field, RIM + start, RIM + start + size, axis=1)

    def send(part):
        return [lax.ppermute(part, "gy", around(count, s)) for s in range(1, count)]

    velocity, part = lax.optimization_barrier((velocity, plane_range(velocity, *cuts[0])))
    arrived = [send(part)]
    velocity, part = lax.optimization_barrier((velocity, plane_range(velocity, *cuts[1])))
    arrived.append(send(part))
    for k, cut in enumerate(cuts[2:]):
        arrived[k], part = lax.optimization_barrier((arrived[k], plane_range(velocity, *cut)))
        arrived.append(send(part))
    operators, arrived[0] = lax.optimization_barrier((operators, arrived[0]))

    inner = lax.slice_in_dim(velocity, RIM, RIM + planes, axis=1)
    left = jnp.swapaxes(lax.slice_in_dim(inner, width - RIM, width, axis=3), 2, 3)
    right = jnp.swapaxes(lax.slice_in_dim(inner, 0, RIM, axis=3), 2, 3)
    left = lax.ppermute(left, "gx", around(ring, ring - 1))
    right = lax.ppermute(right, "gx", around(ring, 1))
    nothing = jnp.zeros((3, planes, 8 - 2 * RIM, rows), jnp.float32)
    halo = jnp.concatenate([left, right, nothing], axis=2)

    block = jnp.where(position >= count // 2, count - 1 - position, position)
    own_columns = lax.dynamic_slice_in_dim(operators, block * rows, rows, axis=2)
    acc = stencils(velocity, halo)
    piece, acc = gather_rows(own_columns, acc)
    weights = column_weights(piece, position, count)

    acc = add_column(acc, weights, 0, [velocity], RIM, 0, planes)
    for (start, size), lines in zip(cuts, arrived):
        acc = add_column(acc, weights, 1, lines, 0, start, size)
    return acc


def solution(mesh):
    placed = (P(None, None, "gy", "gx"), P(None, "gx", None))
    return jax.shard_map(
        shards, mesh=mesh, in_specs=placed, out_specs=P(None, None, "gy", "gx"), check_vma=False
    )
```

```python
import functools

import jax
import jax.numpy as jnp
import numpy as np
from jax import lax
from jax.experimental import pallas as pl
from jax.experimental.pallas import tpu as pltpu
from jax.sharding import PartitionSpec as P

RIM = 3
WEIGHTS = ((1, 45.0), (2, -9.0), (3, 1.0))
CHUNKS = (1, 6, 1)
BRIEF = pl.CostEstimate(flops=1000, bytes_accessed=1000, transcendentals=0)


def stencil_matrices(width):
    inside = np.zeros((width, width), np.float32)
    rim = np.zeros((8, width), np.float32)
    for m in range(width):
        for step, weight in WEIGHTS:
            for offset, signed in ((step, weight), (-step, -weight)):
                at = m + offset
                if at < 0:
                    rim[at + RIM, m] = signed
                elif at >= width:
                    rim[at - width + RIM, m] = signed
                else:
                    inside[at, m] = signed
    return inside, rim


def split(value):
    high = value.astype(jnp.bfloat16)
    low = (value - high.astype(jnp.float32)).astype(jnp.bfloat16)
    return high, low


def dot(left, right, contract=((1,), (0,)), precision=None):
    return lax.dot_general(
        left, right, (contract, ((), ())),
        preferred_element_type=jnp.float32, precision=precision,
    )


def stencil_kernel(vel_ref, halo_ref, inside_ref, rim_ref, out_ref):
    planes = out_ref.shape[1]
    inside = inside_ref[...]
    rim = rim_ref[...]
    for z in range(planes):
        for i in range(3):
            high, low = split(vel_ref[i, RIM + z] * vel_ref[0, RIM + z])
            total = dot(high, inside) + dot(low, inside)
            edges = halo_ref[i, z] * halo_ref[0, z]
            total += dot(edges, rim, ((0,), (0,)), lax.Precision.HIGHEST)
            for step, weight in WEIGHTS:
                up, down = RIM + z + step, RIM + z - step
                total += weight * (
                    vel_ref[i, up] * vel_ref[2, up] - vel_ref[i, down] * vel_ref[2, down]
                )
            out_ref[i, z] = total * (-1.0 / 60.0)


def stencils(velocity, halo):
    _, held, rows, width = velocity.shape
    planes = held - 2 * RIM
    tile = 128 if rows % 128 == 0 else rows
    inside, rim = stencil_matrices(width)
    return pl.pallas_call(
        stencil_kernel,
        grid=(rows // tile,),
        in_specs=[
            pl.BlockSpec((3, held, tile, width), lambda t: (0, 0, t, 0)),
            pl.BlockSpec((3, planes, 8, tile), lambda t: (0, 0, 0, t)),
            pl.BlockSpec((width, width), lambda t: (0, 0)),
            pl.BlockSpec((8, width), lambda t: (0, 0)),
        ],
        out_specs=pl.BlockSpec((3, planes, tile, width), lambda t: (0, 0, t, 0)),
        out_shape=jax.ShapeDtypeStruct((3, planes, rows, width), jnp.float32),
        compiler_params=pltpu.CompilerParams(vmem_limit_bytes=24 << 20),
        cost_estimate=BRIEF,
        name="stencils",
    )(velocity, halo, jnp.asarray(inside, jnp.bfloat16), jnp.asarray(rim))


def flip_or_same(size, flipped):
    row = lax.broadcasted_iota(jnp.int32, (size, size), 0)
    column = lax.broadcasted_iota(jnp.int32, (size, size), 1)
    wanted = jnp.where(flipped == 1, size - 1 - column, column)
    return jnp.where(row == wanted, 1.0, 0.0).astype(jnp.bfloat16)


def weights_kernel(flags, piece_ref, high_ref, low_ref):
    entry = pl.program_id(0) * 4
    block, same, flip_in, flip_out = (flags[entry + k] for k in range(4))
    depth, tile = high_ref.shape[2], high_ref.shape[1]
    strip = piece_ref.shape[3]
    pairs = depth // (2 * strip)
    even, odd = (
        jnp.concatenate(
            [piece_ref[core, block * pairs + r, c] for r in range(pairs) for core in range(2)],
            axis=0,
        )
        for c in range(2)
    )
    combined = even + jnp.where(same == 1, odd, -odd)
    combined = jnp.where(flip_out == 1, combined, -combined)
    turn_in = flip_or_same(depth, flip_in)
    turn_out = flip_or_same(tile, flip_out)
    for part, out_ref in zip(split(combined), (high_ref, low_ref)):
        turned = dot(part, turn_in, ((0,), (0,))).astype(jnp.bfloat16)
        out_ref[0] = dot(turn_out, turned).astype(jnp.bfloat16)


def column_weights(piece, position, count):
    _, pairs, _, strip, rows = piece.shape
    halfway = 2 * pairs * strip
    tile = 256 if rows % 256 == 0 else rows
    tiles = rows // tile
    source = lax.rem(position + jnp.arange(count, dtype=jnp.int32), count)
    low_half = source >= count // 2
    mine = position >= count // 2
    flags = jnp.stack(
        [
            jnp.where(low_half, count - 1 - source, source),
            (low_half == mine).astype(jnp.int32),
            low_half.astype(jnp.int32),
            jnp.broadcast_to(mine, (count,)).astype(jnp.int32),
        ],
        axis=1,
    ).reshape(-1)
    shape = jax.ShapeDtypeStruct((count, rows, rows), jnp.bfloat16)
    out_spec = pl.BlockSpec((1, tile, rows), lambda s, g, flags: (s, g, 0))
    return pl.pallas_call(
        weights_kernel,
        grid_spec=pltpu.PrefetchScalarGridSpec(
            num_scalar_prefetch=1,
            grid=(count, tiles),
            in_specs=[
                pl.BlockSpec(
                    (2, pairs, 2, strip, tile),
                    lambda s, g, flags: (
                        0, 0, 0, 0, jnp.where(flags[s * 4 + 3] == 1, tiles - 1 - g, g)
                    ),
                )
            ],
            out_specs=[out_spec, out_spec],
        ),
        out_shape=[shape, shape],
        compiler_params=pltpu.CompilerParams(vmem_limit_bytes=24 << 20),
        cost_estimate=BRIEF,
        name="weights",
    )(flags, piece)


def column_kernel(first, count, acc_ref, high_ref, low_ref, *refs):
    *lines, out_ref = refs
    total = None
    for s in range(count):
        line = lines[s]
        v = line[1, 0]
        high, low = split(jnp.concatenate([line[i, 0] * v for i in range(3)], axis=1))
        w_high, w_low = high_ref[first + s], low_ref[first + s]
        term = dot(w_high, high) + (dot(w_high, low) + dot(w_low, high))
        total = term if total is None else total + term
    width = out_ref.shape[3]
    for i in range(3):
        out_ref[i, 0] = acc_ref[i, 0] + total[:, i * width:(i + 1) * width]


def add_column(acc, weights, first, lines, offset, start, planes):
    high, low = weights
    _, _, rows, width = acc.shape
    count = len(lines)
    block = (3, 1, rows, width)
    held = pl.BlockSpec(block, lambda z: (0, start + z, 0, 0))
    whole = pl.BlockSpec(high.shape, lambda z: (0, 0, 0), pipeline_mode=pl.Buffered(1))
    if count == 1:
        whole = pl.BlockSpec(
            (1,) + high.shape[1:], lambda z: (first, 0, 0), pipeline_mode=pl.Buffered(1)
        )
        first_in_block = 0
    else:
        first_in_block = first
    return pl.pallas_call(
        functools.partial(column_kernel, first_in_block, count),
        grid=(planes,),
        in_specs=[held, whole, whole]
        + [pl.BlockSpec(block, lambda z: (0, offset + z, 0, 0))] * count,
        out_specs=held,
        out_shape=jax.ShapeDtypeStruct(acc.shape, acc.dtype),
        input_output_aliases={0: 0},
        compiler_params=pltpu.CompilerParams(vmem_limit_bytes=32 << 20),
        cost_estimate=BRIEF,
        name="column",
    )(acc, high, low, *lines)


def around(count, step):
    return [((i + step) % count, i) for i in range(count)]


def gather_rows(block, last):
    ring = lax.axis_size("gx")
    me = lax.axis_index("gx")
    if ring & (ring - 1):
        rows = lax.all_gather(block, "gx", axis=0)
        return jnp.swapaxes(rows.reshape((ring // 2, 2) + block.shape), 0, 1), last

    def exchange(held, bit, join):
        other = lax.ppermute(held, "gx", [(i, i ^ (1 << bit)) for i in range(ring)])
        upper = (me >> bit) & 1 == 1
        return join([jnp.where(upper, other, held), jnp.where(upper, held, other)], 0)

    held = block[None]
    for bit in range(1, ring.bit_length() - 1):
        held = exchange(held, bit, jnp.concatenate)
    held, last = lax.optimization_barrier((held, last))
    return exchange(held, 0, jnp.stack), last


def shards(velocity, operators):
    _, held, rows, width = velocity.shape
    planes = held - 2 * RIM
    ring = lax.axis_size("gx")
    count = lax.axis_size("gy")
    position = lax.axis_index("gy")

    cuts, at = [], 0
    for size in CHUNKS:
        if at < planes:
            cuts.append((at, min(size, planes - at)))
            at += size
    if at < planes:
        cuts.append((at, planes - at))

    def plane_range(field, start, size):
        return lax.slice_in_dim(field, RIM + start, RIM + start + size, axis=1)

    def send(part):
        return [lax.ppermute(part, "gy", around(count, s)) for s in range(1, count)]

    velocity, part = lax.optimization_barrier((velocity, plane_range(velocity, *cuts[0])))
    arrived = [send(part)]
    velocity, part = lax.optimization_barrier((velocity, plane_range(velocity, *cuts[1])))
    arrived.append(send(part))
    for k, cut in enumerate(cuts[2:]):
        arrived[k], part = lax.optimization_barrier((arrived[k], plane_range(velocity, *cut)))
        arrived.append(send(part))
    operators, arrived[0] = lax.optimization_barrier((operators, arrived[0]))

    inner = lax.slice_in_dim(velocity, RIM, RIM + planes, axis=1)
    left = jnp.swapaxes(lax.slice_in_dim(inner, width - RIM, width, axis=3), 2, 3)
    right = jnp.swapaxes(lax.slice_in_dim(inner, 0, RIM, axis=3), 2, 3)
    left = lax.ppermute(left, "gx", around(ring, ring - 1))
    right = lax.ppermute(right, "gx", around(ring, 1))
    nothing = jnp.zeros((3, planes, 8 - 2 * RIM, rows), jnp.float32)
    halo = jnp.concatenate([left, right, nothing], axis=2)

    block = jnp.where(position >= count // 2, count - 1 - position, position)
    own_columns = lax.dynamic_slice_in_dim(operators, block * rows, rows, axis=2)
    acc = stencils(velocity, halo)
    piece, acc = gather_rows(own_columns, acc)
    weights = column_weights(piece, position, count)

    acc = add_column(acc, weights, 0, [velocity], RIM, 0, planes)
    for (start, size), lines in zip(cuts, arrived):
        acc = add_column(acc, weights, 1, lines, 0, start, size)
    return acc


def solution(mesh):
    placed = (P(None, None, "gy", "gx"), P(None, "gx", None))
    return jax.shard_map(
        shards, mesh=mesh, in_specs=placed, out_specs=P(None, None, "gy", "gx"), check_vma=False
    )
```
